32 devices in a mesh: seq: 4 (over z), batch: 4 (over y, x), chan: 2 (over core).
Axes of the slice: x: 2, y: 2, z: 4, core: 2. Of those that a mesh axis runs over, the one named last changes fastest.
Arguments:
- gate_input: bfloat16 [8, 256, 4096], P('batch', 'seq', 'chan'), may hold values from -20 to 20
- key_input: bfloat16 [8, 256, 4096], P('batch', 'seq', 'chan'), may hold values from -6 to 6
- value_input: bfloat16 [8, 256, 4096], P('batch', 'seq', 'chan'), may hold values from -6 to 6
- cotangent: bfloat16 [8, 256, 4096], P('batch', 'seq', 'chan'), may hold values from -6 to 6
- filters: float32 [256, 256], P('chan'), may hold values from -0.75 to 0.75
- document_lengths: int32 [8, 2], P('batch'), may hold values from 1 to 192, 256 in all within a row
Outputs:
- gated_output: bfloat16 [8, 256, 4096], P('batch', 'seq', 'chan')
- gate_gradient: bfloat16 [8, 256, 4096], P('batch', 'seq', 'chan')
- key_gradient: bfloat16 [8, 256, 4096], P('batch', 'seq', 'chan')
- value_gradient: bfloat16 [8, 256, 4096], P('batch', 'seq', 'chan')
- filter_update: float32 [256, 256], P(('seq', 'batch'), 'chan')
The draws below stay inside these ranges and needn't reach their ends.
Inputs may be any that keep to these rules, and one draw needn't show every extreme that they name: `document_lengths`: each row lists, in order, the lengths of the documents packed end to end into one sequence; a row sums to 256.
All inputs are finite; a program needn't handle non-finite values.
Results may differ from the reference program's by a relative error of at most 0.0057.
Values may be sent and summed in bfloat16 or wider, within the bound.
A program may use at most 128 MiB of HBM per device.

```python
import math
import jax
import jax.numpy as jnp
import numpy as np
from jax import lax

D = 4096
GROUPS = 256
SPAN = 64
SEQS = 8
SEQ_LEN = 256
FILT = 256
DOC_MAX = 192
NDOCS = 2
N_SEQ = 4


def draw_gate_input(key, part):
    noise_key = jax.random.fold_in(key, 11)
    scale_key = jax.random.fold_in(key, 12)
    channel = jnp.arange(D, dtype=jnp.float32)
    factor = jnp.exp(jax.random.uniform(scale_key, (D,), minval=-0.69, maxval=0.69))
    scale = 0.25 * jnp.exp(2.302585 * channel / D) * factor
    values = jnp.clip(jax.random.normal(noise_key, (SEQS, SEQ_LEN, D)), -4.0, 4.0)
    return (values * scale[None, None, :]).astype(jnp.bfloat16)


def block_scale(key, shape, shards, least, high):
    loudness, own = 1.0, jax.random.fold_in(key, 6)
    for axis_at, parts in shards:
        heights = jnp.exp(jax.random.uniform(jax.random.fold_in(own, axis_at), (parts,), jnp.float32, least / len(shards), high / len(shards)))
        loudness = loudness * jnp.repeat(heights, shape[axis_at] // parts).reshape([-1 if axis == axis_at else 1 for axis in range(len(shape))])
    return loudness


def profile(amount, total, limit, lean):
    portions = [(1 << 20) // math.isqrt(grade ** lean) + 1 for grade in range(2, amount + 1)]
    surplus, given = total - limit - (amount - 1), [1] * (amount - 1)
    while surplus > 0:
        movable = [i for i in range(amount - 1) if given[i] < limit]
        mass, budget = sum([portions[i] for i in movable]), surplus
        for i in movable:
            extra = min(limit - given[i], max(1, budget * portions[i] // mass), surplus)
            given[i] = given[i] + extra
            surplus = surplus - extra
    return np.array([limit] + given)


def uneven_parts(rng, count, total, reach, lean):
    if count == 2:
        one = jax.random.randint(rng, (), max(1, total - reach), min(reach, total - 1) + 1)
        return jnp.stack([one, total - one])
    sizes = jnp.asarray(profile(count, total, reach, lean), jnp.int32)
    couples = (count - 1) // 2
    giver, taker = sizes[1:1 + 2 * couples:2], sizes[2:2 + 2 * couples:2]
    slack = jnp.minimum(giver - 1, reach - taker)
    shifted = jax.random.randint(jax.random.fold_in(rng, 1), (couples,), 0, 1 << 20) % (slack + 1)
    sizes = sizes.at[1:1 + 2 * couples:2].set(giver - shifted).at[2:2 + 2 * couples:2].set(taker + shifted)
    return sizes[jax.random.permutation(jax.random.fold_in(rng, 2), count)]


def centred(rng, extent, scale, most, split=(), kind=jnp.bfloat16):
    drawn = jax.random.normal(rng, extent, jnp.float32) * scale
    if len(split) > 0:
        drawn = block_scale(rng, extent, split, -0.22, 0.18) * drawn
    return jnp.clip(drawn, min=-most, max=most).astype(kind)


def setup_inputs(seed: int = 0) -> dict:
    key_of = jax.random.split(jax.random.key(seed), 7)
    return {
        "gate_input": draw_gate_input(jax.random.fold_in(key_of[6], 71), 0),
        "key_input": centred(key_of[1], (SEQS, SEQ_LEN, D), 1.0, 6.0, ((0, 4), (1, 4), (2, 2))),
        "value_input": centred(key_of[2], (SEQS, SEQ_LEN, D), 1.0, 6.0, ((0, 4), (1, 4), (2, 2))),
        "cotangent": centred(key_of[3], (SEQS, SEQ_LEN, D), 1.0, 6.0, ((0, 4), (1, 4), (2, 2))),
        "filters": centred(key_of[4], (GROUPS, FILT), SPAN ** -0.5, 0.75, ((0, 2),), jnp.float32),
        "document_lengths": jax.vmap(lambda own: uneven_parts(own, NDOCS, SEQ_LEN, DOC_MAX, 2))(jax.random.split(key_of[5], SEQS)).reshape((SEQS, NDOCS)).astype(jnp.int32),
    }


reach_blocks = 5

def span_documents(lengths, index):
    rows = jnp.arange(SPAN, dtype=jnp.int32)
    positions = index * SPAN + rows
    ends = jnp.cumsum(lengths)
    documents = lax.optimization_barrier(jnp.sum((positions[:, None] >= ends[None, :]).astype(jnp.int32), axis=1))
    inside = (positions >= 0) & (positions < SEQ_LEN)
    return (positions, documents, inside)

def pair_keep(lengths, target, source):
    target_positions, target_documents, target_in = span_documents(lengths, target)
    source_positions, source_documents, source_in = span_documents(lengths, source)
    keep = (target_documents[:, None] == source_documents[None, :]) & target_in[:, None] & source_in[None, :]
    keep = keep & (source_positions[None, :] <= target_positions[:, None])
    return keep.astype(jnp.float32)

def reference(gate_input, key_input, value_input, cotangent, filters, document_lengths):
    members = D // GROUPS
    rounded_filters = lax.optimization_barrier(filters.astype(jnp.bfloat16)).astype(jnp.float32)
    rows = jnp.arange(SPAN, dtype=jnp.int32)

    def toeplitz(lag):
        taps = lag * SPAN + rows[:, None] - rows[None, :]
        valid = (taps >= 0) & (taps < FILT)
        picked = jnp.take(rounded_filters, jnp.clip(taps, 0, FILT - 1), axis=1)
        return jnp.where(valid[None], picked, 0.0)
    blocks = jnp.stack([toeplitz(lag) for lag in range(reach_blocks)])
    units = (key_input.astype(jnp.float32) * value_input.astype(jnp.float32)).astype(jnp.bfloat16)
    gated_cotangent = (cotangent.astype(jnp.float32) * gate_input.astype(jnp.float32)).astype(jnp.bfloat16)
    margin = (reach_blocks - 1) * SPAN

    def per_sequence(operands):
        unit_seq, cotangent_seq, lengths = operands
        unit_pad = jnp.pad(unit_seq.astype(jnp.float32), ((margin, margin), (0, 0))).reshape(-1, GROUPS, members)
        cotangent_pad = jnp.pad(cotangent_seq.astype(jnp.float32), ((margin, margin), (0, 0))).reshape(-1, GROUPS, members)

        def per_span(index):
            own = lax.dynamic_slice_in_dim(cotangent_pad, index * SPAN + margin, SPAN, 0)
            forward = jnp.zeros((SPAN, GROUPS, members), jnp.float32)
            backward = jnp.zeros((SPAN, GROUPS, members), jnp.float32)
            tap_sums = jnp.zeros((FILT, GROUPS), jnp.float32)
            for lag in range(reach_blocks):
                block = blocks[lag]
                source = lax.dynamic_slice_in_dim(unit_pad, (index - lag) * SPAN + margin, SPAN, 0)
                later = lax.dynamic_slice_in_dim(cotangent_pad, (index + lag) * SPAN + margin, SPAN, 0)
                keep_forward = pair_keep(lengths, index, index - lag)
                keep_backward = pair_keep(lengths, index + lag, index)
                forward = forward + jnp.einsum('gij,jgm->igm', block * keep_forward[None], source)
                backward = backward + jnp.einsum('gij,igm->jgm', block * keep_backward[None], later)
                paired = jnp.einsum('igm,jgm->ijg', own, source) * keep_forward[:, :, None]
                taps = (lag * SPAN + rows[:, None] - rows[None, :]).reshape(-1)
                tap_sums = tap_sums + jax.ops.segment_sum(paired.reshape(SPAN * SPAN, GROUPS), jnp.clip(taps, 0, FILT - 1), num_segments=FILT)
            return (forward, backward, tap_sums)
        forward, backward, tap_sums = lax.map(per_span, jnp.arange(N_SEQ, dtype=jnp.int32))
        return (forward.reshape(SEQ_LEN, D), backward.reshape(SEQ_LEN, D), lax.optimization_barrier(jnp.sum(tap_sums, axis=0)))
    filtered, adjoint, sums = lax.map(per_sequence, (units, gated_cotangent, document_lengths))
    filter_sums = lax.optimization_barrier(jnp.sum(sums, axis=0))
    root_mean = jnp.sqrt(jnp.mean(filter_sums * filter_sums) + 1e-06)
    filter_update = filter_sums * jnp.minimum(1.0, 1.0 / root_mean)
    gated_output = (gate_input.astype(jnp.float32) * filtered).astype(jnp.bfloat16)
    gate_gradient = (cotangent.astype(jnp.float32) * filtered).astype(jnp.bfloat16)
    key_gradient = (adjoint * value_input.astype(jnp.float32)).astype(jnp.bfloat16)
    value_gradient = (adjoint * key_input.astype(jnp.float32)).astype(jnp.bfloat16)
    return (gated_output, gate_gradient, key_gradient, value_gradient, filter_update)
```

```python
import functools

import jax
import jax.numpy as jnp
from jax import lax
from jax.experimental import pallas as pl
from jax.experimental.pallas import tpu as pltpu
from jax.sharding import PartitionSpec as P

MESH = pl.DeviceIdType.MESH
LANES = 128


def kernel(
    dims, gate, key, value, cotangent, filters, lengths,
    gated_output, gate_gradient, key_gradient, value_gradient, filter_update,
    units, followers, reversed_own, plain, flipped, forward_block, backward_block,
    forward_mask, backward_mask, sums_mask, tap_sums, shares_out, shares_in, squares_out, squares_in,
    unit_send, unit_recv, cot_send, cot_recv, share_send, share_recv, square_send, square_recv,
):
    n_seq, n_batch, n_chan, reach, wide, chunks, tiles, seqs, span, groups, taps, ndocs = dims
    everyone = n_seq * n_batch * n_chan
    sharers = n_seq * n_batch
    here = lax.axis_index("seq")
    batch = lax.axis_index("batch")
    chan = lax.axis_index("chan")
    me = (here * n_batch + batch) * n_chan + chan
    mine = here * n_batch + batch
    per_tile = LANES * groups // (tiles * chunks * LANES)
    members = LANES // per_tile
    lanes = tiles * LANES
    own = reach * span

    barrier = pltpu.get_barrier_semaphore()

    rest = wide - own - span
    for c in range(chunks):
        for s in range(seqs):
            units[c, s, pl.ds(0, own), :] = jnp.zeros((own, lanes), jnp.bfloat16)
            units[c, s, pl.ds(own + span, rest), :] = jnp.zeros((rest, lanes), jnp.bfloat16)
            followers[c, s, pl.ds(span, wide - span), :] = jnp.zeros((wide - span, lanes), jnp.bfloat16)

    def greet(i, carry):
        other = lax.rem(me + i, everyone)
        pl.semaphore_signal(
            barrier, inc=1, device_id_type=MESH,
            device_id={
                "seq": other // (n_batch * n_chan),
                "batch": lax.rem(other // n_chan, n_batch),
                "chan": lax.rem(other, n_chan),
            },
        )
        return carry

    lax.fori_loop(1, everyone, greet, 0)

    for c in range(chunks):
        at = pl.ds(c * lanes, lanes)
        for s in range(seqs):
            u = (key[s, :, at].astype(jnp.float32) * value[s, :, at].astype(jnp.float32)).astype(jnp.bfloat16)
            g = (cotangent[s, :, at].astype(jnp.float32) * gate[s, :, at].astype(jnp.float32)).astype(jnp.bfloat16)
            units[c, s, pl.ds(own, span), :] = u
            followers[c, s, pl.ds(0, span), :] = g

    def unit_copy(lag, c):
        source = units.at[c, :, pl.ds((reach - lag + 1) * span, span), :]
        target = units.at[c, :, pl.ds((reach - lag) * span, span), :]
        return pltpu.make_async_remote_copy(
            src_ref=source, dst_ref=target, send_sem=unit_send.at[lag - 1, c], recv_sem=unit_recv.at[lag - 1, c],
            device_id={"seq": here + 1}, device_id_type=MESH,
        )

    def cot_copy(lag, c):
        source = followers.at[c, :, pl.ds((lag - 1) * span, span), :]
        target = followers.at[c, :, pl.ds(lag * span, span), :]
        return pltpu.make_async_remote_copy(
            src_ref=source, dst_ref=target, send_sem=cot_send.at[lag - 1, c], recv_sem=cot_recv.at[lag - 1, c],
            device_id={"seq": here - 1}, device_id_type=MESH,
        )

    def sends_up(lag):
        return (here >= lag - 1) & (here + 1 < n_seq)

    def sends_down(lag):
        return (here + lag - 1 < n_seq) & (here >= 1)

    def send(lag, c):
        @pl.when(sends_up(lag))
        def _():
            unit_copy(lag, c).start()

        @pl.when(sends_down(lag))
        def _():
            cot_copy(lag, c).start()

    def receive(lag, c):
        @pl.when(here >= lag)
        def _():
            unit_copy(lag, c).wait_recv()

        @pl.when(here + lag < n_seq)
        def _():
            cot_copy(lag, c).wait_recv()

    pl.semaphore_wait(barrier, everyone - 1)
    for c in range(chunks):
        send(1, c)

    def documents(positions, s):
        count = jnp.zeros(positions.shape, jnp.int32)
        end = 0
        for n in range(ndocs):
            end = end + lengths[s, n]
            count = count + (positions >= end).astype(jnp.int32)
        return count

    rows = lax.broadcasted_iota(jnp.int32, (span, 1), 0)
    cols = lax.broadcasted_iota(jnp.int32, (1, wide), 1)
    for s in range(seqs):
        earlier = (here - reach) * span + cols
        later = here * span + cols
        target = here * span + rows
        back = here * span + (span - 1 - rows)
        earlier_doc = documents(earlier, s)
        later_doc = documents(later, s)
        target_doc = documents(target, s)
        back_doc = documents(back, s)
        keep = (earlier_doc == target_doc) & (earlier <= target) & (earlier >= 0)
        forward_mask[s] = jnp.where(keep, 1.0, 0.0).astype(jnp.bfloat16)
        keep = (earlier_doc == back_doc) & (earlier <= back) & (earlier >= 0)
        sums_mask[s] = jnp.where(keep, 1.0, 0.0)
        keep = (later_doc == target_doc) & (later >= target) & (later < n_seq * span)
        backward_mask[s] = jnp.where(keep, 1.0, 0.0).astype(jnp.bfloat16)

    rounded = filters[...].astype(jnp.bfloat16)
    a = lax.broadcasted_iota(jnp.int32, (taps, wide), 0)
    b = lax.broadcasted_iota(jnp.int32, (taps, wide), 1)
    flip = own - b
    flip = jnp.where(flip < 0, flip + wide, flip)
    plain[...] = jnp.dot(rounded, jnp.where(a == b, 1.0, 0.0).astype(jnp.bfloat16), preferred_element_type=jnp.float32)
    flipped[...] = jnp.dot(rounded, jnp.where(a == flip, 1.0, 0.0).astype(jnp.bfloat16), preferred_element_type=jnp.float32)

    def build(t, carry):
        for i in range(per_tile):
            g = t * per_tile + i
            at = pl.ds(pl.multiple_of(g * span, span), span)
            row = jnp.broadcast_to(flipped[pl.ds(g, 1), :], (span, wide))
            forward_block[at, :] = pltpu.roll(row, 0, 1, stride=1, stride_axis=0).astype(jnp.bfloat16)
            row = jnp.broadcast_to(plain[pl.ds(g, 1), :], (span, wide))
            backward_block[at, :] = pltpu.roll(row, 0, 1, stride=1, stride_axis=0).astype(jnp.bfloat16)
        return carry

    order_a = lax.broadcasted_iota(jnp.int32, (span, span), 0)
    order_b = lax.broadcasted_iota(jnp.int32, (span, span), 1)
    exchange = jnp.where(order_a + order_b == span - 1, 1.0, 0.0).astype(jnp.bfloat16)
    for c in range(chunks):
        lax.fori_loop(c * tiles, (c + 1) * tiles, build, 0)
        for s in range(seqs):
            reversed_own[c, s] = jnp.dot(
                exchange, followers[c, s, pl.ds(0, span), :], preferred_element_type=jnp.float32
            ).astype(jnp.bfloat16)
        for lag in range(1, reach):
            receive(lag, c)
            send(lag + 1, c)

    lane = lax.broadcasted_iota(jnp.int32, (1, LANES), 1) // members

    def paired(c, j, carry):
        at = pl.ds(pl.multiple_of(j * LANES, LANES), LANES)
        total = None
        for s in range(seqs):
            source = units[c, s, :, at]
            target = reversed_own[c, s, :, at]
            stacked = jnp.concatenate(
                [target * jnp.where(lane == i, 1.0, 0.0).astype(jnp.bfloat16) for i in range(per_tile)], axis=0
            )
            products = lax.dot_general(
                stacked, source, (((1,), (1,)), ((), ())), preferred_element_type=jnp.float32
            ).reshape(per_tile, span, wide)
            products = products * sums_mask[s][None]
            total = products if total is None else total + products
        for i in range(per_tile):
            aligned = pltpu.roll(total[i], 0, 1, stride=1, stride_axis=0)
            tap_sums[pl.ds((c * tiles + j) * per_tile + i, 1), :] = jnp.sum(aligned, axis=0, keepdims=True)
        return carry

    for c in range(chunks):
        receive(reach, c)
        lax.fori_loop(0, tiles, functools.partial(paired, c), 0)

    a = lax.broadcasted_iota(jnp.int32, (taps, wide), 0)
    b = lax.broadcasted_iota(jnp.int32, (taps, wide), 1)
    pick = jnp.where(a + b == own + span - 1, 1.0, 0.0)
    by_tap = lax.dot_general(
        pick, tap_sums[...], (((1,), (1,)), ((), ())),
        precision=lax.Precision.HIGHEST, preferred_element_type=jnp.float32,
    )
    share = taps // sharers
    for i in range(sharers):
        shares_out[i] = by_tap[i * share : (i + 1) * share, :]

    def share_copy(i):
        other = lax.rem(mine + i, sharers)
        return pltpu.make_async_remote_copy(
            src_ref=shares_out.at[other], dst_ref=shares_in.at[i - 1],
            send_sem=share_send.at[i - 1], recv_sem=share_recv.at[i - 1],
            device_id={"seq": other // n_batch, "batch": lax.rem(other, n_batch)}, device_id_type=MESH,
        )

    def square_copy(i):
        other = lax.rem(me + i, everyone)
        return pltpu.make_async_remote_copy(
            src_ref=squares_out, dst_ref=squares_in.at[i - 1],
            send_sem=square_send.at[i - 1], recv_sem=square_recv.at[i - 1],
            device_id={
                "seq": other // (n_batch * n_chan),
                "batch": lax.rem(other // n_chan, n_batch),
                "chan": lax.rem(other, n_chan),
            },
            device_id_type=MESH,
        )

    def loop(low, high, act):
        def step(i, carry):
            act(i)
            return carry

        lax.fori_loop(low, high, step, 0)

    def convolve(c, j, carry):
        at = pl.ds(pl.multiple_of(j * LANES, LANES), LANES)
        t = c * tiles + j
        out = pl.ds(pl.multiple_of(t * LANES, LANES), LANES)
        height = per_tile * span
        block = pl.ds(pl.multiple_of(t * height, height), height)

        def apply(block_ref, mask_ref, data_ref, s):
            masked = block_ref[block, :].reshape(per_tile, span, wide) * mask_ref[s][None]
            results = jnp.dot(
                masked.reshape(height, wide), data_ref[c, s, :, at], preferred_element_type=jnp.float32
            )
            picked = results[:span]
            for i in range(1, per_tile):
                picked = jnp.where(lane == i, results[i * span : (i + 1) * span], picked)
            return picked

        for s in range(seqs):
            filtered = apply(forward_block, forward_mask, units, s)
            gated_output[s, :, out] = (gate[s, :, out].astype(jnp.float32) * filtered).astype(jnp.bfloat16)
            gate_gradient[s, :, out] = (cotangent[s, :, out].astype(jnp.float32) * filtered).astype(jnp.bfloat16)
            adjoint = apply(backward_block, backward_mask, followers, s)
            key_gradient[s, :, out] = (adjoint * value[s, :, out].astype(jnp.float32)).astype(jnp.bfloat16)
            value_gradient[s, :, out] = (adjoint * key[s, :, out].astype(jnp.float32)).astype(jnp.bfloat16)
        return carry

    loop(1, sharers, lambda i: share_copy(i).start())
    half = chunks // 2
    for c in range(half):
        lax.fori_loop(0, tiles, functools.partial(convolve, c), 0)
    loop(1, sharers, lambda i: share_copy(i).wait_recv())
    total = shares_out[mine] + jnp.sum(shares_in[...], axis=0)
    squares_out[...] = jnp.sum(total * total, axis=0, keepdims=True)
    filter_update[...] = total
    for c in range(half, half + 1):
        lax.fori_loop(0, 1, functools.partial(convolve, c), 0)
    loop(1, everyone, lambda i: square_copy(i).start())
    for c in range(half, chunks):
        lax.fori_loop(1 if c == half else 0, tiles, functools.partial(convolve, c), 0)
    loop(1, everyone, lambda i: square_copy(i).wait_recv())
    squares = jnp.sum(squares_in[...], axis=0) + squares_out[...]
    mean = jnp.sum(squares, axis=1, keepdims=True) / (taps * groups * n_chan)
    filter_update[...] = filter_update[...] * jnp.minimum(1.0, 1.0 / jnp.sqrt(mean + 1e-06))

    loop(1, sharers, lambda i: share_copy(i).wait_send())
    loop(1, everyone, lambda i: square_copy(i).wait_send())
    for lag in range(1, reach + 1):
        @pl.when(sends_up(lag))
        def _():
            for c in range(chunks):
                unit_copy(lag, c).wait_send()

        @pl.when(sends_down(lag))
        def _():
            for c in range(chunks):
                cot_copy(lag, c).wait_send()


def per_device(sizes, gate_input, key_input, value_input, cotangent, filters, document_lengths):
    n_seq, n_batch, n_chan = sizes
    seqs, span, width = gate_input.shape
    groups, taps = filters.shape
    ndocs = document_lengths.shape[1]
    longest = min(taps, n_seq * span - span)
    reach = (longest - 1) // span if ndocs == 2 else (longest - 2) // span + 1
    wide = -(-((reach + 2) * span - 1) // LANES) * LANES
    chunks = 4
    tiles = width // (chunks * LANES)
    lanes = tiles * LANES
    sharers = n_seq * n_batch
    everyone = sharers * n_chan
    share = taps // sharers
    dims = (n_seq, n_batch, n_chan, reach, wide, chunks, tiles, seqs, span, groups, taps, ndocs)
    bf16, f32 = jnp.bfloat16, jnp.float32
    vmem = pl.BlockSpec(memory_space=pltpu.VMEM)
    dma = pltpu.SemaphoreType.DMA
    like = jax.ShapeDtypeStruct(gate_input.shape, bf16)
    return pl.pallas_call(
        functools.partial(kernel, dims),
        out_shape=(like, like, like, like, jax.ShapeDtypeStruct((share, groups), f32)),
        in_specs=[vmem] * 5 + [pl.BlockSpec(memory_space=pltpu.SMEM)],
        out_specs=(vmem,) * 5,
        scratch_shapes=[
            pltpu.VMEM((chunks, seqs, wide, lanes), bf16),
            pltpu.VMEM((chunks, seqs, wide, lanes), bf16),
            pltpu.VMEM((chunks, seqs, span, lanes), bf16),
            pltpu.VMEM((groups, wide), f32),
            pltpu.VMEM((groups, wide), f32),
            pltpu.VMEM((groups * span, wide), bf16),
            pltpu.VMEM((groups * span, wide), bf16),
            pltpu.VMEM((seqs, span, wide), bf16),
            pltpu.VMEM((seqs, span, wide), bf16),
            pltpu.VMEM((seqs, span, wide), f32),
            pltpu.VMEM((groups, wide), f32),
            pltpu.VMEM((sharers, share, groups), f32),
            pltpu.VMEM((sharers - 1, share, groups), f32),
            pltpu.VMEM((1, groups), f32),
            pltpu.VMEM((everyone - 1, 1, groups), f32),
            dma((reach, chunks)), dma((reach, chunks)), dma((reach, chunks)), dma((reach, chunks)),
            dma((sharers - 1,)), dma((sharers - 1,)), dma((everyone - 1,)), dma((everyone - 1,)),
        ],
        compiler_params=pltpu.CompilerParams(
            collective_id=0, has_side_effects=True, vmem_limit_bytes=60 * 1024 * 1024
        ),
    )(gate_input, key_input, value_input, cotangent, filters, document_lengths)


def solution(mesh):
    block = P("batch", "seq", "chan")
    sizes = (mesh.shape["seq"], mesh.shape["batch"], mesh.shape["chan"])
    return jax.shard_map(
        functools.partial(per_device, sizes),
        mesh=mesh,
        in_specs=(block, block, block, block, P("chan", None), P("batch", None)),
        out_specs=(block, block, block, block, P(("seq", "batch"), "chan")),
        check_vma=False,
    )
```

```python
import functools

import jax
import jax.numpy as jnp
from jax import lax
from jax.experimental import pallas as pl
from jax.experimental.pallas import tpu as pltpu
from jax.sharding import PartitionSpec as P

MESH = pl.DeviceIdType.MESH
LANES = 128
HELD = 4
SHARES_AT = 4


def kernel(
    dims, gate, key, value, cotangent, filters, lengths,
    gated_output, gate_gradient, key_gradient, value_gradient, filter_update,
    units, followers, reversed_own, plain, flipped, forward_block, backward_block,
    forward_mask, backward_mask, sums_mask, tap_sums, shares_out, shares_in, squares_out, squares_in,
    chan_out, chan_in,
    unit_send, unit_recv, cot_send, cot_recv, share_send, share_recv, square_send, square_recv,
    chan_send, chan_recv,
):
    n_seq, n_batch, n_chan, reach, wide, chunks, tiles, seqs, span, groups, taps, ndocs = dims
    everyone = n_seq * n_batch * n_chan
    sharers = n_seq * n_batch
    here = lax.axis_index("seq")
    batch = lax.axis_index("batch")
    chan = lax.axis_index("chan")
    me = (here * n_batch + batch) * n_chan + chan
    mine = here * n_batch + batch
    per_tile = LANES * groups // (tiles * chunks * LANES)
    members = LANES // per_tile
    lanes = tiles * LANES
    own = reach * span
    hub = reach == 2

    barrier = pltpu.get_barrier_semaphore()

    rest = wide - own - span
    for c in range(chunks):
        for s in range(seqs):
            units[c, s, pl.ds(0, own), :] = jnp.zeros((own, lanes), jnp.bfloat16)
            units[c, s, pl.ds(own + span, rest), :] = jnp.zeros((rest, lanes), jnp.bfloat16)
            followers[c, s, pl.ds(span, wide - span), :] = jnp.zeros((wide - span, lanes), jnp.bfloat16)

    def greet(i, carry):
        other = lax.rem(me + i, everyone)
        pl.semaphore_signal(
            barrier, inc=1, device_id_type=MESH,
            device_id={
                "seq": other // (n_batch * n_chan),
                "batch": lax.rem(other // n_chan, n_batch),
                "chan": lax.rem(other, n_chan),
            },
        )
        return carry

    lax.fori_loop(1, everyone, greet, 0)

    for c in range(chunks):
        at = pl.ds(c * lanes, lanes)
        for s in range(seqs):
            u = (key[s, :, at].astype(jnp.float32) * value[s, :, at].astype(jnp.float32)).astype(jnp.bfloat16)
            g = (cotangent[s, :, at].astype(jnp.float32) * gate[s, :, at].astype(jnp.float32)).astype(jnp.bfloat16)
            units[c, s, pl.ds(own, span), :] = u
            followers[c, s, pl.ds(0, span), :] = g

    def unit_copy(lag, c):
        source = units.at[c, :, pl.ds((reach - lag + 1) * span, span), :]
        target = units.at[c, :, pl.ds((reach - lag) * span, span), :]
        return pltpu.make_async_remote_copy(
            src_ref=source, dst_ref=target, send_sem=unit_send.at[lag - 1, c], recv_sem=unit_recv.at[lag - 1, c],
            device_id={"seq": here + 1}, device_id_type=MESH,
        )

    def cot_copy(lag, c):
        source = followers.at[c, :, pl.ds((lag - 1) * span, span), :]
        target = followers.at[c, :, pl.ds(lag * span, span), :]
        return pltpu.make_async_remote_copy(
            src_ref=source, dst_ref=target, send_sem=cot_send.at[lag - 1, c], recv_sem=cot_recv.at[lag - 1, c],
            device_id={"seq": here - 1}, device_id_type=MESH,
        )

    def sends_up(lag):
        return (here >= lag - 1) & (here + 1 < n_seq)

    def sends_down(lag):
        return (here + lag - 1 < n_seq) & (here >= 1)

    def send(lag, c):
        @pl.when(sends_up(lag))
        def _():
            unit_copy(lag, c).start()

        @pl.when(sends_down(lag))
        def _():
            cot_copy(lag, c).start()

    def receive(lag, c):
        @pl.when(here >= lag)
        def _():
            unit_copy(lag, c).wait_recv()

        @pl.when(here + lag < n_seq)
        def _():
            cot_copy(lag, c).wait_recv()

    pl.semaphore_wait(barrier, everyone - 1)
    for c in range(chunks):
        send(1, c)

    def documents(positions, s):
        count = jnp.zeros(positions.shape, jnp.int32)
        end = 0
        for n in range(ndocs):
            end = end + lengths[s, n]
            count = count + (positions >= end).astype(jnp.int32)
        return count

    rows = lax.broadcasted_iota(jnp.int32, (span, 1), 0)
    cols = lax.broadcasted_iota(jnp.int32, (1, wide), 1)
    for s in range(seqs):
        earlier = (here - reach) * span + cols
        later = here * span + cols
        target = here * span + rows
        back = here * span + (span - 1 - rows)
        earlier_doc = documents(earlier, s)
        later_doc = documents(later, s)
        target_doc = documents(target, s)
        back_doc = documents(back, s)
        keep = (earlier_doc == target_doc) & (earlier <= target) & (earlier >= 0)
        forward_mask[s] = jnp.where(keep, 1.0, 0.0).astype(jnp.bfloat16)
        if hub:
            first = cols < span
            origin = jnp.where(first, earlier + span, earlier)
            goal = jnp.where(first, back + span, back)
            goal_doc = jnp.where(first, documents(back + span, s), back_doc)
            keep = (documents(origin, s) == goal_doc) & (origin <= goal) & (origin >= 0) & (goal < n_seq * span)
        else:
            keep = (earlier_doc == back_doc) & (earlier <= back) & (earlier >= 0)
        sums_mask[s] = jnp.where(keep, 1.0, 0.0)
        keep = (later_doc == target_doc) & (later >= target) & (later < n_seq * span)
        backward_mask[s] = jnp.where(keep, 1.0, 0.0).astype(jnp.bfloat16)

    rounded = filters[...].astype(jnp.bfloat16)
    a = lax.broadcasted_iota(jnp.int32, (taps, wide), 0)
    b = lax.broadcasted_iota(jnp.int32, (taps, wide), 1)
    flip = own - b
    flip = jnp.where(flip < 0, flip + wide, flip)
    plain[...] = jnp.dot(rounded, jnp.where(a == b, 1.0, 0.0).astype(jnp.bfloat16), preferred_element_type=jnp.float32)
    flipped[...] = jnp.dot(rounded, jnp.where(a == flip, 1.0, 0.0).astype(jnp.bfloat16), preferred_element_type=jnp.float32)

    def build(t, carry):
        for i in range(per_tile):
            g = t * per_tile + i
            at = pl.ds(pl.multiple_of(g * span, span), span)
            row = jnp.broadcast_to(flipped[pl.ds(g, 1), :], (span, wide))
            forward_block[at, :] = pltpu.roll(row, 0, 1, stride=1, stride_axis=0).astype(jnp.bfloat16)
            row = jnp.broadcast_to(plain[pl.ds(g, 1), :], (span, wide))
            backward_block[at, :] = pltpu.roll(row, 0, 1, stride=1, stride_axis=0).astype(jnp.bfloat16)
        return carry

    order_a = lax.broadcasted_iota(jnp.int32, (span, span), 0)
    order_b = lax.broadcasted_iota(jnp.int32, (span, span), 1)
    exchange = jnp.where(order_a + order_b == span - 1, 1.0, 0.0).astype(jnp.bfloat16)
    lane = lax.broadcasted_iota(jnp.int32, (1, LANES), 1) // members

    def members_apart(block):
        return jnp.concatenate(
            [block * jnp.where(lane == i, 1.0, 0.0).astype(jnp.bfloat16) for i in range(per_tile)], axis=0
        )

    def paired(c, j, carry):
        at = pl.ds(pl.multiple_of(j * LANES, LANES), LANES)
        total = None
        for s in range(seqs):
            target = members_apart(reversed_own[c, s, pl.ds(0, span), at])
            if hub:
                target = jnp.concatenate([target, members_apart(reversed_own[c, s, pl.ds(span, span), at])], axis=1)
                past = units[c, s, pl.ds(own - span, span), at]
                blank = jnp.zeros((span, LANES), jnp.bfloat16)
                tail = jnp.zeros((wide - own - span, LANES), jnp.bfloat16)
                source = jnp.concatenate(
                    [
                        jnp.concatenate([blank, past, units[c, s, pl.ds(own, span), at], tail], axis=0),
                        jnp.concatenate([past, blank, blank, tail], axis=0),
                    ],
                    axis=1,
                )
            else:
                source = units[c, s, :, at]
            products = lax.dot_general(
                target, source, (((1,), (1,)), ((), ())), preferred_element_type=jnp.float32
            ).reshape(per_tile, span, wide)
            products = products * sums_mask[s][None]
            total = products if total is None else total + products
        for i in range(per_tile):
            aligned = pltpu.roll(total[i], 0, 1, stride=1, stride_axis=0)
            tap_sums[pl.ds((c * tiles + j) * per_tile + i, 1), :] = jnp.sum(aligned, axis=0, keepdims=True)
        return carry

    def reverse(c):
        for s in range(seqs):
            for n in range(2 if hub else 1):
                at = pl.ds(n * span, span)
                reversed_own[c, s, at, :] = jnp.dot(
                    exchange, followers[c, s, at, :], preferred_element_type=jnp.float32
                ).astype(jnp.bfloat16)

    for c in range(chunks):
        lax.fori_loop(c * tiles, (c + 1) * tiles, build, 0)
        for lag in range(1, reach):
            receive(lag, c)
            if not (hub and c >= HELD):
                send(lag + 1, c)
        if hub:
            reverse(c)
            lax.fori_loop(0, tiles, functools.partial(paired, c), 0)
    if not hub:
        for c in range(chunks):
            receive(reach, c)
            reverse(c)
            lax.fori_loop(0, tiles, functools.partial(paired, c), 0)

    a = lax.broadcasted_iota(jnp.int32, (taps, wide), 0)
    b = lax.broadcasted_iota(jnp.int32, (taps, wide), 1)
    pick = jnp.where(a + b == own + span - 1, 1.0, 0.0)
    by_tap = lax.dot_general(
        pick, tap_sums[...], (((1,), (1,)), ((), ())),
        precision=lax.Precision.HIGHEST, preferred_element_type=jnp.float32,
    )
    share = taps // sharers
    for i in range(sharers):
        shares_out[i] = by_tap[i * share : (i + 1) * share, :]

    def share_copy(i):
        other = lax.rem(mine + i, sharers)
        return pltpu.make_async_remote_copy(
            src_ref=shares_out.at[other], dst_ref=shares_in.at[i - 1],
            send_sem=share_send.at[i - 1], recv_sem=share_recv.at[i - 1],
            device_id={"seq": other // n_batch, "batch": lax.rem(other, n_batch)}, device_id_type=MESH,
        )

    def square_copy(i):
        other = lax.rem(mine + i, sharers)
        return pltpu.make_async_remote_copy(
            src_ref=squares_out, dst_ref=squares_in.at[i - 1],
            send_sem=square_send.at[i - 1], recv_sem=square_recv.at[i - 1],
            device_id={"seq": other // n_batch, "batch": lax.rem(other, n_batch)}, device_id_type=MESH,
        )

    def chan_copy(i):
        return pltpu.make_async_remote_copy(
            src_ref=chan_out, dst_ref=chan_in.at[i - 1],
            send_sem=chan_send.at[i - 1], recv_sem=chan_recv.at[i - 1],
            device_id={"chan": lax.rem(chan + i, n_chan)}, device_id_type=MESH,
        )

    def loop(low, high, act):
        if high <= 32:
            for i in range(low, high):
                act(i)
            return

        def step(i, carry):
            act(i)
            return carry

        lax.fori_loop(low, high, step, 0)

    def convolve(c, j, carry):
        at = pl.ds(pl.multiple_of(j * LANES, LANES), LANES)
        t = c * tiles + j
        out = pl.ds(pl.multiple_of(t * LANES, LANES), LANES)
        height = per_tile * span
        block = pl.ds(pl.multiple_of(t * height, height), height)

        def apply(block_ref, mask_ref, data_ref, s):
            masked = block_ref[block, :].reshape(per_tile, span, wide) * mask_ref[s][None]
            results = jnp.dot(
                masked.reshape(height, wide), data_ref[c, s, :, at], preferred_element_type=jnp.float32
            )
            picked = results[:span]
            for i in range(1, per_tile):
                picked = jnp.where(lane == i, results[i * span : (i + 1) * span], picked)
            return picked

        for s in range(seqs):
            filtered = apply(forward_block, forward_mask, units, s)
            gated_output[s, :, out] = (gate[s, :, out].astype(jnp.float32) * filtered).astype(jnp.bfloat16)
            gate_gradient[s, :, out] = (cotangent[s, :, out].astype(jnp.float32) * filtered).astype(jnp.bfloat16)
            adjoint = apply(backward_block, backward_mask, followers, s)
            key_gradient[s, :, out] = (adjoint * value[s, :, out].astype(jnp.float32)).astype(jnp.bfloat16)
            value_gradient[s, :, out] = (adjoint * key[s, :, out].astype(jnp.float32)).astype(jnp.bfloat16)
        return carry

    loop(1, sharers, lambda i: share_copy(i).start())
    if hub:
        for c in range(HELD, chunks):
            send(reach, c)
    for c in range(chunks):
        if hub:
            receive(reach, c)
        if c == SHARES_AT:
            loop(1, sharers, lambda i: share_copy(i).wait_recv())
            total = shares_out[mine] + jnp.sum(shares_in[...], axis=0)
            filter_update[...] = total
            squares_out[...] = jnp.sum(total * total, axis=0, keepdims=True)
        if c == SHARES_AT + 1:
            loop(1, sharers, lambda i: square_copy(i).start())
        lax.fori_loop(0, tiles, functools.partial(convolve, c), 0)
    loop(1, sharers, lambda i: square_copy(i).wait_recv())
    chan_out[...] = jnp.sum(squares_in[...], axis=0) + squares_out[...]
    loop(1, sharers, lambda i: share_copy(i).wait_send())
    loop(1, sharers, lambda i: square_copy(i).wait_send())
    loop(1, n_chan, lambda i: chan_copy(i).start())
    loop(1, n_chan, lambda i: chan_copy(i).wait_recv())
    squares = jnp.sum(chan_in[...], axis=0) + chan_out[...]
    mean = jnp.sum(squares, axis=1, keepdims=True) / (taps * groups * n_chan)
    filter_update[...] = filter_update[...] * jnp.minimum(1.0, 1.0 / jnp.sqrt(mean + 1e-06))
    loop(1, n_chan, lambda i: chan_copy(i).wait_send())
    for lag in range(1, reach + 1):
        @pl.when(sends_up(lag))
        def _():
            for c in range(chunks):
                unit_copy(lag, c).wait_send()

        @pl.when(sends_down(lag))
        def _():
            for c in range(chunks):
                cot_copy(lag, c).wait_send()


def per_device(sizes, gate_input, key_input, value_input, cotangent, filters, document_lengths):
    n_seq, n_batch, n_chan = sizes
    seqs, span, width = gate_input.shape
    groups, taps = filters.shape
    ndocs = document_lengths.shape[1]
    longest = min(taps, n_seq * span - span)
    reach = (longest - 1) // span if ndocs == 2 else (longest - 2) // span + 1
    wide = -(-((reach + 2) * span - 1) // LANES) * LANES
    chunks = 8
    tiles = width // (chunks * LANES)
    lanes = tiles * LANES
    sharers = n_seq * n_batch
    share = taps // sharers
    dims = (n_seq, n_batch, n_chan, reach, wide, chunks, tiles, seqs, span, groups, taps, ndocs)
    bf16, f32 = jnp.bfloat16, jnp.float32
    vmem = pl.BlockSpec(memory_space=pltpu.VMEM)
    dma = pltpu.SemaphoreType.DMA
    like = jax.ShapeDtypeStruct(gate_input.shape, bf16)
    return pl.pallas_call(
        functools.partial(kernel, dims),
        out_shape=(like, like, like, like, jax.ShapeDtypeStruct((share, groups), f32)),
        in_specs=[vmem] * 5 + [pl.BlockSpec(memory_space=pltpu.SMEM)],
        out_specs=(vmem,) * 5,
        scratch_shapes=[
            pltpu.VMEM((chunks, seqs, wide, lanes), bf16),
            pltpu.VMEM((chunks, seqs, wide, lanes), bf16),
            pltpu.VMEM((chunks, seqs, 2 * span, lanes), bf16),
            pltpu.VMEM((groups, wide), f32),
            pltpu.VMEM((groups, wide), f32),
            pltpu.VMEM((groups * span, wide), bf16),
            pltpu.VMEM((groups * span, wide), bf16),
            pltpu.VMEM((seqs, span, wide), bf16),
            pltpu.VMEM((seqs, span, wide), bf16),
            pltpu.VMEM((seqs, span, wide), f32),
            pltpu.VMEM((groups, wide), f32),
            pltpu.VMEM((sharers, share, groups), f32),
            pltpu.VMEM((sharers - 1, share, groups), f32),
            pltpu.VMEM((1, groups), f32),
            pltpu.VMEM((sharers - 1, 1, groups), f32),
            pltpu.VMEM((1, groups), f32),
            pltpu.VMEM((n_chan - 1, 1, groups), f32),
            dma((reach, chunks)), dma((reach, chunks)), dma((reach, chunks)), dma((reach, chunks)),
            dma((sharers - 1,)), dma((sharers - 1,)), dma((sharers - 1,)), dma((sharers - 1,)),
            dma((n_chan - 1,)), dma((n_chan - 1,)),
        ],
        compiler_params=pltpu.CompilerParams(
            collective_id=0, has_side_effects=True, vmem_limit_bytes=60 * 1024 * 1024
        ),
    )(gate_input, key_input, value_input, cotangent, filters, document_lengths)


def solution(mesh):
    block = P("batch", "seq", "chan")
    sizes = (mesh.shape["seq"], mesh.shape["batch"], mesh.shape["chan"])
    return jax.shard_map(
        functools.partial(per_device, sizes),
        mesh=mesh,
        in_specs=(block, block, block, block, P("chan", None), P("batch", None)),
        out_specs=(block, block, block, block, P(("seq", "batch"), "chan")),
        check_vma=False,
    )
```

```python
import functools

import jax
import jax.numpy as jnp
from jax import lax
from jax.experimental import pallas as pl
from jax.experimental.pallas import tpu as pltpu
from jax.sharding import PartitionSpec as P

MESH = pl.DeviceIdType.MESH
LANES = 128
HELD = 4
SHARES_AT = 3


def kernel(
    dims, gate, key, value, cotangent, filters, lengths,
    gated_output, gate_gradient, key_gradient, value_gradient, filter_update,
    units, followers, reversed_own, plain, flipped, forward_block, backward_block,
    forward_mask, backward_mask, sums_mask, tap_sums, shares_out, shares_in, squares_out, squares_in,
    chan_out, chan_in,
    unit_send, unit_recv, cot_send, cot_recv, share_send, share_recv, square_send, square_recv,
    chan_send, chan_recv,
):
    n_seq, n_batch, n_chan, reach, wide, chunks, tiles, seqs, span, groups, taps, ndocs = dims
    everyone = n_seq * n_batch * n_chan
    sharers = n_seq * n_batch
    here = lax.axis_index("seq")
    batch = lax.axis_index("batch")
    chan = lax.axis_index("chan")
    me = (here * n_batch + batch) * n_chan + chan
    mine = here * n_batch + batch
    per_tile = LANES * groups // (tiles * chunks * LANES)
    members = LANES // per_tile
    lanes = tiles * LANES
    own = reach * span
    hub = reach == 2

    barrier = pltpu.get_barrier_semaphore()

    rest = wide - own - span
    for c in range(chunks):
        for s in range(seqs):
            units[c, s, pl.ds(0, own), :] = jnp.zeros((own, lanes), jnp.bfloat16)
            units[c, s, pl.ds(own + span, rest), :] = jnp.zeros((rest, lanes), jnp.bfloat16)
            followers[c, s, pl.ds(span, wide - span), :] = jnp.zeros((wide - span, lanes), jnp.bfloat16)

    def greet(i, carry):
        other = lax.rem(me + i, everyone)
        pl.semaphore_signal(
            barrier, inc=1, device_id_type=MESH,
            device_id={
                "seq": other // (n_batch * n_chan),
                "batch": lax.rem(other // n_chan, n_batch),
                "chan": lax.rem(other, n_chan),
            },
        )
        return carry

    lax.fori_loop(1, everyone, greet, 0)

    def unit_copy(lag, c):
        source = units.at[c, :, pl.ds((reach - lag + 1) * span, span), :]
        target = units.at[c, :, pl.ds((reach - lag) * span, span), :]
        return pltpu.make_async_remote_copy(
            src_ref=source, dst_ref=target, send_sem=unit_send.at[lag - 1, c], recv_sem=unit_recv.at[lag - 1, c],
            device_id={"seq": here + 1}, device_id_type=MESH,
        )

    def cot_copy(lag, c):
        source = followers.at[c, :, pl.ds((lag - 1) * span, span), :]
        target = followers.at[c, :, pl.ds(lag * span, span), :]
        return pltpu.make_async_remote_copy(
            src_ref=source, dst_ref=target, send_sem=cot_send.at[lag - 1, c], recv_sem=cot_recv.at[lag - 1, c],
            device_id={"seq": here - 1}, device_id_type=MESH,
        )

    def sends_up(lag):
        return (here >= lag - 1) & (here + 1 < n_seq)

    def sends_down(lag):
        return (here + lag - 1 < n_seq) & (here >= 1)

    def send(lag, c):
        @pl.when(sends_up(lag))
        def _():
            unit_copy(lag, c).start()

        @pl.when(sends_down(lag))
        def _():
            cot_copy(lag, c).start()

    def receive(lag, c):
        @pl.when(here >= lag)
        def _():
            unit_copy(lag, c).wait_recv()

        @pl.when(here + lag < n_seq)
        def _():
            cot_copy(lag, c).wait_recv()

    def load(c):
        at = pl.ds(c * lanes, lanes)
        for s in range(seqs):
            u = (key[s, :, at].astype(jnp.float32) * value[s, :, at].astype(jnp.float32)).astype(jnp.bfloat16)
            g = (cotangent[s, :, at].astype(jnp.float32) * gate[s, :, at].astype(jnp.float32)).astype(jnp.bfloat16)
            units[c, s, pl.ds(own, span), :] = u
            followers[c, s, pl.ds(0, span), :] = g

    load(0)
    pl.semaphore_wait(barrier, everyone - 1)
    for c in range(chunks):
        if c + 1 < chunks:
            load(c + 1)
        send(1, c)

    def documents(positions, s):
        count = jnp.zeros(positions.shape, jnp.int32)
        end = 0
        for n in range(ndocs):
            end = end + lengths[s, n]
            count = count + (positions >= end).astype(jnp.int32)
        return count

    rows = lax.broadcasted_iota(jnp.int32, (span, 1), 0)
    cols = lax.broadcasted_iota(jnp.int32, (1, wide), 1)
    for s in range(seqs):
        earlier = (here - reach) * span + cols
        later = here * span + cols
        target = here * span + rows
        back = here * span + (span - 1 - rows)
        earlier_doc = documents(earlier, s)
        later_doc = documents(later, s)
        target_doc = documents(target, s)
        back_doc = documents(back, s)
        keep = (earlier_doc == target_doc) & (earlier <= target) & (earlier >= 0)
        forward_mask[s] = jnp.where(keep, 1.0, 0.0).astype(jnp.bfloat16)
        if hub:
            first = cols < span
            origin = jnp.where(first, earlier + span, earlier)
            goal = jnp.where(first, back + span, back)
            goal_doc = jnp.where(first, documents(back + span, s), back_doc)
            keep = (documents(origin, s) == goal_doc) & (origin <= goal) & (origin >= 0) & (goal < n_seq * span)
        else:
            keep = (earlier_doc == back_doc) & (earlier <= back) & (earlier >= 0)
        sums_mask[s] = jnp.where(keep, 1.0, 0.0)
        keep = (later_doc == target_doc) & (later >= target) & (later < n_seq * span)
        backward_mask[s] = jnp.where(keep, 1.0, 0.0).astype(jnp.bfloat16)

    rounded = filters[...].astype(jnp.bfloat16)
    a = lax.broadcasted_iota(jnp.int32, (taps, wide), 0)
    b = lax.broadcasted_iota(jnp.int32, (taps, wide), 1)
    flip = own - b
    flip = jnp.where(flip < 0, flip + wide, flip)
    plain[...] = jnp.dot(rounded, jnp.where(a == b, 1.0, 0.0).astype(jnp.bfloat16), preferred_element_type=jnp.float32)
    flipped[...] = jnp.dot(rounded, jnp.where(a == flip, 1.0, 0.0).astype(jnp.bfloat16), preferred_element_type=jnp.float32)

    def build(t, carry):
        for i in range(per_tile):
            g = t * per_tile + i
            at = pl.ds(pl.multiple_of(g * span, span), span)
            row = jnp.broadcast_to(flipped[pl.ds(g, 1), :], (span, wide))
            forward_block[at, :] = pltpu.roll(row, 0, 1, stride=1, stride_axis=0).astype(jnp.bfloat16)
            row = jnp.broadcast_to(plain[pl.ds(g, 1), :], (span, wide))
            backward_block[at, :] = pltpu.roll(row, 0, 1, stride=1, stride_axis=0).astype(jnp.bfloat16)
        return carry

    order_a = lax.broadcasted_iota(jnp.int32, (span, span), 0)
    order_b = lax.broadcasted_iota(jnp.int32, (span, span), 1)
    exchange = jnp.where(order_a + order_b == span - 1, 1.0, 0.0).astype(jnp.bfloat16)
    lane = lax.broadcasted_iota(jnp.int32, (1, LANES), 1) // members

    def members_apart(block):
        return jnp.concatenate(
            [block * jnp.where(lane == i, 1.0, 0.0).astype(jnp.bfloat16) for i in range(per_tile)], axis=0
        )

    def paired(c, j, carry):
        at = pl.ds(pl.multiple_of(j * LANES, LANES), LANES)
        total = None
        for s in range(seqs):
            target = members_apart(reversed_own[c, s, pl.ds(0, span), at])
            if hub:
                target = jnp.concatenate([target, members_apart(reversed_own[c, s, pl.ds(span, span), at])], axis=1)
                past = units[c, s, pl.ds(own - span, span), at]
                blank = jnp.zeros((span, LANES), jnp.bfloat16)
                tail = jnp.zeros((wide - own - span, LANES), jnp.bfloat16)
                source = jnp.concatenate(
                    [
                        jnp.concatenate([blank, past, units[c, s, pl.ds(own, span), at], tail], axis=0),
                        jnp.concatenate([past, blank, blank, tail], axis=0),
                    ],
                    axis=1,
                )
            else:
                source = units[c, s, :, at]
            products = lax.dot_general(
                target, source, (((1,), (1,)), ((), ())), preferred_element_type=jnp.float32
            ).reshape(per_tile, span, wide)
            products = products * sums_mask[s][None]
            total = products if total is None else total + products
        for i in range(per_tile):
            aligned = pltpu.roll(total[i], 0, 1, stride=1, stride_axis=0)
            tap_sums[pl.ds((c * tiles + j) * per_tile + i, 1), :] = jnp.sum(aligned, axis=0, keepdims=True)
        return carry

    def reverse(c):
        for s in range(seqs):
            for n in range(2 if hub else 1):
                at = pl.ds(n * span, span)
                reversed_own[c, s, at, :] = jnp.dot(
                    exchange, followers[c, s, at, :], preferred_element_type=jnp.float32
                ).astype(jnp.bfloat16)

    for c in range(chunks):
        lax.fori_loop(c * tiles, (c + 1) * tiles, build, 0)
        for lag in range(1, reach):
            receive(lag, c)
            if not (hub and c >= HELD):
                send(lag + 1, c)
        if hub:
            reverse(c)
            lax.fori_loop(0, tiles, functools.partial(paired, c), 0)
    if not hub:
        for c in range(chunks):
            receive(reach, c)
            reverse(c)
            lax.fori_loop(0, tiles, functools.partial(paired, c), 0)

    a = lax.broadcasted_iota(jnp.int32, (taps, wide), 0)
    b = lax.broadcasted_iota(jnp.int32, (taps, wide), 1)
    pick = jnp.where(a + b == own + span - 1, 1.0, 0.0)
    by_tap = lax.dot_general(
        pick, tap_sums[...], (((1,), (1,)), ((), ())),
        precision=lax.Precision.HIGHEST, preferred_element_type=jnp.float32,
    )
    share = taps // sharers
    for i in range(sharers):
        shares_out[i] = by_tap[i * share : (i + 1) * share, :]

    def share_copy(i):
        other = lax.rem(mine + i, sharers)
        return pltpu.make_async_remote_copy(
            src_ref=shares_out.at[other], dst_ref=shares_in.at[i - 1],
            send_sem=share_send.at[i - 1], recv_sem=share_recv.at[i - 1],
            device_id={"seq": other // n_batch, "batch": lax.rem(other, n_batch)}, device_id_type=MESH,
        )

    def square_copy(i):
        other = lax.rem(mine + i, sharers)
        return pltpu.make_async_remote_copy(
            src_ref=squares_out, dst_ref=squares_in.at[i - 1],
            send_sem=square_send.at[i - 1], recv_sem=square_recv.at[i - 1],
            device_id={"seq": other // n_batch, "batch": lax.rem(other, n_batch)}, device_id_type=MESH,
        )

    def chan_copy(i):
        return pltpu.make_async_remote_copy(
            src_ref=chan_out, dst_ref=chan_in.at[i - 1],
            send_sem=chan_send.at[i - 1], recv_sem=chan_recv.at[i - 1],
            device_id={"chan": lax.rem(chan + i, n_chan)}, device_id_type=MESH,
        )

    def loop(low, high, act):
        if high <= 32:
            for i in range(low, high):
                act(i)
            return

        def step(i, carry):
            act(i)
            return carry

        lax.fori_loop(low, high, step, 0)

    def convolve(c, j, carry):
        at = pl.ds(pl.multiple_of(j * LANES, LANES), LANES)
        t = c * tiles + j
        out = pl.ds(pl.multiple_of(t * LANES, LANES), LANES)
        height = per_tile * span
        block = pl.ds(pl.multiple_of(t * height, height), height)

        def apply(block_ref, mask_ref, data_ref, s):
            masked = block_ref[block, :].reshape(per_tile, span, wide) * mask_ref[s][None]
            results = jnp.dot(
                masked.reshape(height, wide), data_ref[c, s, :, at], preferred_element_type=jnp.float32
            )
            picked = results[:span]
            for i in range(1, per_tile):
                picked = jnp.where(lane == i, results[i * span : (i + 1) * span], picked)
            return picked

        for s in range(seqs):
            filtered = apply(forward_block, forward_mask, units, s)
            gated_output[s, :, out] = (gate[s, :, out].astype(jnp.float32) * filtered).astype(jnp.bfloat16)
            gate_gradient[s, :, out] = (cotangent[s, :, out].astype(jnp.float32) * filtered).astype(jnp.bfloat16)
            adjoint = apply(backward_block, backward_mask, followers, s)
            key_gradient[s, :, out] = (adjoint * value[s, :, out].astype(jnp.float32)).astype(jnp.bfloat16)
            value_gradient[s, :, out] = (adjoint * key[s, :, out].astype(jnp.float32)).astype(jnp.bfloat16)
        return carry

    loop(1, sharers, lambda i: share_copy(i).start())
    if hub:
        for c in range(HELD, chunks):
            send(reach, c)
    for c in range(chunks):
        if hub:
            receive(reach, c)
        if c == SHARES_AT:
            loop(1, sharers, lambda i: share_copy(i).wait_recv())
            total = shares_out[mine] + jnp.sum(shares_in[...], axis=0)
            filter_update[...] = total
            squares_out[...] = jnp.sum(total * total, axis=0, keepdims=True)
        if c == SHARES_AT + 1:
            loop(1, sharers, lambda i: square_copy(i).start())
        lax.fori_loop(0, tiles, functools.partial(convolve, c), 0)
    loop(1, sharers, lambda i: square_copy(i).wait_recv())
    chan_out[...] = jnp.sum(squares_in[...], axis=0) + squares_out[...]
    loop(1, sharers, lambda i: share_copy(i).wait_send())
    loop(1, sharers, lambda i: square_copy(i).wait_send())
    loop(1, n_chan, lambda i: chan_copy(i).start())
    loop(1, n_chan, lambda i: chan_copy(i).wait_recv())
    squares = jnp.sum(chan_in[...], axis=0) + chan_out[...]
    mean = jnp.sum(squares, axis=1, keepdims=True) / (taps * groups * n_chan)
    filter_update[...] = filter_update[...] * jnp.minimum(1.0, 1.0 / jnp.sqrt(mean + 1e-06))
    loop(1, n_chan, lambda i: chan_copy(i).wait_send())
    for lag in range(1, reach + 1):
        @pl.when(sends_up(lag))
        def _():
            for c in range(chunks):
                unit_copy(lag, c).wait_send()

        @pl.when(sends_down(lag))
        def _():
            for c in range(chunks):
                cot_copy(lag, c).wait_send()


def per_device(sizes, gate_input, key_input, value_input, cotangent, filters, document_lengths):
    n_seq, n_batch, n_chan = sizes
    seqs, span, width = gate_input.shape
    groups, taps = filters.shape
    ndocs = document_lengths.shape[1]
    longest = min(taps, n_seq * span - span)
    reach = (longest - 1) // span if ndocs == 2 else (longest - 2) // span + 1
    wide = -(-((reach + 2) * span - 1) // LANES) * LANES
    chunks = 8
    tiles = width // (chunks * LANES)
    lanes = tiles * LANES
    sharers = n_seq * n_batch
    share = taps // sharers
    dims = (n_seq, n_batch, n_chan, reach, wide, chunks, tiles, seqs, span, groups, taps, ndocs)
    bf16, f32 = jnp.bfloat16, jnp.float32
    vmem = pl.BlockSpec(memory_space=pltpu.VMEM)
    dma = pltpu.SemaphoreType.DMA
    like = jax.ShapeDtypeStruct(gate_input.shape, bf16)
    return pl.pallas_call(
        functools.partial(kernel, dims),
        out_shape=(like, like, like, like, jax.ShapeDtypeStruct((share, groups), f32)),
        in_specs=[vmem] * 5 + [pl.BlockSpec(memory_space=pltpu.SMEM)],
        out_specs=(vmem,) * 5,
        scratch_shapes=[
            pltpu.VMEM((chunks, seqs, wide, lanes), bf16),
            pltpu.VMEM((chunks, seqs, wide, lanes), bf16),
            pltpu.VMEM((chunks, seqs, 2 * span, lanes), bf16),
            pltpu.VMEM((groups, wide), f32),
            pltpu.VMEM((groups, wide), f32),
            pltpu.VMEM((groups * span, wide), bf16),
            pltpu.VMEM((groups * span, wide), bf16),
            pltpu.VMEM((seqs, span, wide), bf16),
            pltpu.VMEM((seqs, span, wide), bf16),
            pltpu.VMEM((seqs, span, wide), f32),
            pltpu.VMEM((groups, wide), f32),
            pltpu.VMEM((sharers, share, groups), f32),
            pltpu.VMEM((sharers - 1, share, groups), f32),
            pltpu.VMEM((1, groups), f32),
            pltpu.VMEM((sharers - 1, 1, groups), f32),
            pltpu.VMEM((1, groups), f32),
            pltpu.VMEM((n_chan - 1, 1, groups), f32),
            dma((reach, chunks)), dma((reach, chunks)), dma((reach, chunks)), dma((reach, chunks)),
            dma((sharers - 1,)), dma((sharers - 1,)), dma((sharers - 1,)), dma((sharers - 1,)),
            dma((n_chan - 1,)), dma((n_chan - 1,)),
        ],
        compiler_params=pltpu.CompilerParams(
            collective_id=0, has_side_effects=True, vmem_limit_bytes=60 * 1024 * 1024
        ),
    )(gate_input, key_input, value_input, cotangent, filters, document_lengths)


def solution(mesh):
    block = P("batch", "seq", "chan")
    sizes = (mesh.shape["seq"], mesh.shape["batch"], mesh.shape["chan"])
    return jax.shard_map(
        functools.partial(per_device, sizes),
        mesh=mesh,
        in_specs=(block, block, block, block, P("chan", None), P("batch", None)),
        out_specs=(block, block, block, block, P(("seq", "batch"), "chan")),
        check_vma=False,
    )
```
